32 devices in a mesh: grp: 2 (over x), gx: 16 (over z, y, core).
Axes of the slice: x: 2, y: 2, z: 4, core: 2. Of those that a mesh axis runs over, the one named last changes fastest.
Arguments:
- prompt_rows: bfloat16 [4096, 16384], P(('grp', 'gx')), parts along dimension 0, may hold values from -6 to 6
- decode_rows: bfloat16 [64, 16384], P(('grp', 'gx')), parts along dimension 0, may hold values from -6 to 6
- norm_gain: bfloat16 [16384], replicated, may hold values from 0.25 to 1.75
- w_query: bfloat16 [16384, 8192], P(None, 'gx'), may hold values from -0.046875 to 0.046875
- w_key: bfloat16 [16384, 512], P('gx'), may hold values from -0.046875 to 0.046875
- w_value: bfloat16 [16384, 512], P('gx'), may hold values from -0.046875 to 0.046875
- key_cache: bfloat16 [64, 4, 256, 128], P(('grp', 'gx')), parts along dimension 0, may hold values from -6 to 6
- value_cache: bfloat16 [64, 4, 256, 128], P(('grp', 'gx')), parts along dimension 0, may hold values from -6 to 6
- positions: int32 [4096], P(('grp', 'gx')), parts along dimension 0, may hold values from 0 to 8191, as said below
- lengths: int32 [64], P('grp'), parts along dimension 0, may hold values from 1 to 256, 3276 in all
- slots: int32 [32], P('grp'), parts along dimension 0, may hold values from 0 to 31, as said below
Outputs:
- prompt_keys: bfloat16 [4096, 512], P(('grp', 'gx')), parts along dimension 0
- attended: bfloat16 [64, 8192], P(('grp', 'gx')), parts along dimension 0
The draws below stay inside these ranges and needn't reach their ends.
There are 2 independent parts, one for each index of `grp`. The reference program is written for one: setup_inputs(seed, part) draws one part's arguments, and reference() takes and returns one part's arrays. A program takes and returns all parts, laid end to end along the dimension named above; an argument that names none is the same for every part. Nothing has to cross between parts.
Inputs may be any that keep to these rules, and one draw needn't show every extreme that they name: The positions of each span are consecutive. The slots are distinct.
All inputs are finite; a program needn't handle non-finite values.
Results may differ from the reference program's by a relative error of at most 0.007.
Values may be sent and summed in bfloat16 or wider, within the bound.
No kernel may reach another device: no remote copies, remote signals or barrier semaphores. Data moves between devices by JAX's collectives and lax.ppermute only.
A program may use at most 128 MiB of HBM per device.

```python
import math
import jax
import jax.numpy as jnp
import numpy as np
from jax import lax

D = 16384
HEADS = 64
KVH = 4
HD = 128
SPAN = 128
CTX = 256
POSMAX = 8192
TOKENS = 2048
SPANS = 16
DEC = 32


def draw_positions(key, part):
    start_key = jax.random.fold_in(key, 11)
    order_key = jax.random.fold_in(key, 12)
    starts = jax.random.randint(start_key, (SPANS,), 0, POSMAX - SPAN + 1)
    order = jax.random.permutation(order_key, SPANS)
    starts = starts.at[order[0]].set(POSMAX - SPAN)
    starts = starts.at[order[1]].set(0)
    places = starts[:, None] + jnp.arange(SPAN)[None, :]
    return places.reshape(-1).astype(jnp.int32)


def draw_slots(key, part):
    inner_key = jax.random.fold_in(key, 21)
    place_key = jax.random.fold_in(key, 22)
    inner = 1 + jax.random.permutation(inner_key, DEC - 2)[:SPANS - 2]
    chosen = jnp.concatenate([jnp.array([0, DEC - 1], dtype=jnp.int32), inner.astype(jnp.int32)])
    order = jax.random.permutation(place_key, SPANS)
    return chosen[order].astype(jnp.int32)


def block_levels(own_key, extent, split, least, top_value):
    level, own = 1.0, jax.random.fold_in(own_key, 6)
    for axis_at, shards_of in split:
        steps = jnp.exp(jax.random.uniform(jax.random.fold_in(own, axis_at), (shards_of,), jnp.float32, least / len(split), top_value / len(split)))
        level = level * jnp.repeat(steps, extent[axis_at] // shards_of).reshape([-1 if axis == axis_at else 1 for axis in range(len(extent))])
    return level


def length_profile(amount, total, limit, skew):
    weights = [(1 << 20) // math.isqrt(standing ** skew) + 1 for standing in range(2, amount + 1)]
    spare, holding = total - limit - (amount - 1), [1] * (amount - 1)
    while spare > 0:
        movable = [i for i in range(amount - 1) if holding[i] < limit]
        whole, left = sum([weights[i] for i in movable]), spare
        for i in movable:
            addition = min(limit - holding[i], max(1, left * weights[i] // whole), spare)
            holding[i] = holding[i] + addition
            spare = spare - addition
    return np.array([limit] + holding)


def uneven_parts(rng, number_of, total, reach, slope):
    if number_of == 2:
        one = jax.random.randint(rng, (), max(1, total - reach), min(reach, total - 1) + 1)
        return jnp.stack([one, total - one])
    sizes = jnp.asarray(length_profile(number_of, total, reach, slope), jnp.int32)
    couples = (number_of - 1) // 2
    giver, receiver = sizes[1:1 + 2 * couples:2], sizes[2:2 + 2 * couples:2]
    slack = jnp.minimum(giver - 1, reach - receiver)
    moved = jax.random.randint(jax.random.fold_in(rng, 1), (couples,), 0, 1 << 20) % (slack + 1)
    sizes = sizes.at[1:1 + 2 * couples:2].set(giver - moved).at[2:2 + 2 * couples:2].set(receiver + moved)
    return sizes[jax.random.permutation(jax.random.fold_in(rng, 2), number_of)]


def bell_draw(rng, extent, spread, limit, pieces=(), kind=jnp.bfloat16):
    entries = jax.random.normal(rng, extent, jnp.float32) * spread
    if len(pieces) > 0:
        entries = block_levels(rng, extent, pieces, -0.22, 0.18) * entries
    return jnp.clip(entries, min=-limit, max=limit).astype(kind)


def setup_inputs(seed: int = 0, part: int = 0) -> dict:
    key_list = jax.random.split(jax.random.key(seed), 12)
    part_splits = jax.random.split(jax.random.fold_in(key_list[11], part), 12)
    return {
        "prompt_rows": bell_draw(part_splits[0], (TOKENS, D), 1.0, 6.0, ((0, 16),)),
        "decode_rows": bell_draw(part_splits[1], (DEC, D), 1.0, 6.0, ((0, 16),)),
        "norm_gain": jnp.clip(1.0 + 0.15 * jax.random.normal(key_list[2], (D,), jnp.float32), 0.25, 1.75).astype(jnp.bfloat16),
        "w_query": bell_draw(key_list[3], (D, HEADS * HD), D ** -0.5, 0.046875, ((1, 16),)),
        "w_key": bell_draw(key_list[4], (D, KVH * HD), D ** -0.5, 0.046875, ((0, 16),)),
        "w_value": bell_draw(key_list[5], (D, KVH * HD), D ** -0.5, 0.046875, ((0, 16),)),
        "key_cache": bell_draw(part_splits[6], (DEC, KVH, CTX, HD), 1.0, 6.0, ((0, 16),)),
        "value_cache": bell_draw(part_splits[7], (DEC, KVH, CTX, HD), 1.0, 6.0, ((0, 16),)),
        "positions": draw_positions(jax.random.fold_in(jax.random.fold_in(key_list[11], part), 71), part),
        "lengths": uneven_parts(part_splits[9], DEC, 2 * DEC * CTX // 5, CTX, 1).astype(jnp.int32),
        "slots": draw_slots(jax.random.fold_in(jax.random.fold_in(key_list[11], part), 71), part),
    }


THETA = 500000.0
EPSILON = 1e-05

def normalize(values, gain):
    wide = values.astype(jnp.float32)
    square_mean = lax.optimization_barrier(jnp.mean(wide * wide, axis=-1, keepdims=True))
    return (wide * lax.rsqrt(square_mean + EPSILON) * gain.astype(jnp.float32)).astype(jnp.bfloat16)

def rotate(vectors, places):
    head_size = vectors.shape[-1]
    half_size = head_size // 2
    exponent = jnp.arange(half_size).astype(jnp.float32) * (2.0 / head_size)
    inverse = jnp.power(jnp.float32(THETA), -exponent)
    angles = places.astype(jnp.float32)[:, None] * inverse[None, :]
    cosine = jnp.cos(angles)[:, None, :]
    sine = jnp.sin(angles)[:, None, :]
    first = vectors[..., :half_size]
    second = vectors[..., half_size:]
    return jnp.concatenate([first * cosine - second * sine, second * cosine + first * sine], axis=-1)

def reference(prompt_rows, decode_rows, norm_gain, w_query, w_key, w_value, key_cache, value_cache, positions, lengths, slots):
    prompt_normed = normalize(prompt_rows, norm_gain)
    key_raw = jnp.dot(prompt_normed, w_key, preferred_element_type=jnp.float32).reshape(TOKENS, KVH, HD)
    prompt_keys = rotate(key_raw, positions).reshape(TOKENS, KVH * HD).astype(jnp.bfloat16)
    decode_normed = normalize(decode_rows, norm_gain)
    finals = prompt_normed[SPAN - 1::SPAN]
    decode_normed = decode_normed.at[slots].set(finals)
    query_raw = jnp.dot(decode_normed, w_query, preferred_element_type=jnp.float32).reshape(DEC, HEADS, HD)
    queries = rotate(query_raw, lengths).astype(jnp.bfloat16)
    fresh_key_raw = jnp.dot(decode_normed, w_key, preferred_element_type=jnp.float32).reshape(DEC, KVH, HD)
    new_keys = rotate(fresh_key_raw, lengths).astype(jnp.bfloat16)
    new_values = jnp.dot(decode_normed, w_value, preferred_element_type=jnp.float32).reshape(DEC, KVH, HD).astype(jnp.bfloat16)
    grouped = queries.astype(jnp.float32).reshape(DEC, KVH, HEADS // KVH, HD)
    scale_factor = 1.0 / math.sqrt(HD)
    scores = jnp.einsum('bgqd,bgtd->bgqt', grouped, key_cache.astype(jnp.float32)) * scale_factor
    own_scores = jnp.einsum('bgqd,bgd->bgq', grouped, new_keys.astype(jnp.float32)) * scale_factor
    live = jnp.arange(CTX).astype(jnp.int32)[None, :] < lengths[:, None]
    weights = jnp.where(live[:, None, None, :], jnp.exp(scores), jnp.float32(0.0))
    own_weight = jnp.exp(own_scores)
    total = lax.optimization_barrier(jnp.sum(weights, axis=-1)) + own_weight
    shares = (weights / total[..., None]).astype(jnp.bfloat16)
    own_share = (own_weight / total).astype(jnp.bfloat16)
    mixed = jnp.einsum('bgqt,bgtd->bgqd', shares.astype(jnp.float32), value_cache.astype(jnp.float32))
    mixed = mixed + own_share.astype(jnp.float32)[..., None] * new_values.astype(jnp.float32)[:, :, None, :]
    attended = mixed.reshape(DEC, HEADS * HD).astype(jnp.bfloat16)
    return (prompt_keys, attended)
```

```python
import functools
import math

import jax
import jax.numpy as jnp
from jax import lax
from jax.experimental import pallas as pl
from jax.experimental.pallas import tpu as pltpu
from jax.sharding import PartitionSpec as P

THETA = 500000.0
EPSILON = 1e-05
LANES = 128
CORES = 2
PLANE = 4
BOTH = ("grp", "gx")


class Grid:
    def __init__(self, mesh, shard_rows):
        self.parts = mesh.shape["grp"]
        self.count = mesh.shape["gx"]
        self.ys = max(1, PLANE // self.parts)
        self.zs = self.count // (self.ys * CORES)
        pair = self.parts % 2 == 0 and shard_rows % (2 * LANES) == 0
        self.pair = 2 if pair else 1
        self.sub = shard_rows // self.pair

    def place(self, g, z, y, c):
        return g * self.count + (z * self.ys + y) * CORES + c

    def perm(self, dg=0, dz=0, dy=0, dc=0):
        moves = []
        for g in range(self.parts):
            low = g % self.pair
            other = g - low + (low + dg) % self.pair
            for z in range(self.zs):
                for y in range(self.ys):
                    for c in range(CORES):
                        there = self.place(
                            other, (z + dz) % self.zs, (y + dy) % self.ys, (c + dc) % CORES
                        )
                        moves.append((self.place(g, z, y, c), there))
        return moves

    def send(self, value, **offsets):
        return lax.ppermute(value, BOTH, self.perm(**offsets))


def normalize(values, gain):
    wide = values.astype(jnp.float32)
    square_mean = jnp.mean(wide * wide, axis=-1, keepdims=True)
    return (wide * lax.rsqrt(square_mean + EPSILON) * gain.astype(jnp.float32)).astype(jnp.bfloat16)


def angles_of(places, head_size):
    half_size = head_size // 2
    exponent = jnp.arange(half_size).astype(jnp.float32) * (2.0 / head_size)
    inverse = jnp.power(jnp.float32(THETA), -exponent)
    angles = places.astype(jnp.float32)[:, None] * inverse[None, :]
    cosine, sine = jnp.cos(angles), jnp.sin(angles)
    return jnp.concatenate([cosine, cosine], -1), jnp.concatenate([-sine, sine], -1)


def rotate(vectors, cosine, sine):
    half_size = vectors.shape[-1] // 2
    swapped = jnp.concatenate([vectors[..., half_size:], vectors[..., :half_size]], axis=-1)
    return vectors * cosine[:, None, :] + swapped * sine[:, None, :]


def attend(grouped, key_block, value_block, fresh_keys, fresh_values, live_lengths):
    scale_factor = 1.0 / math.sqrt(grouped.shape[-1])
    scores = (
        jnp.einsum("bgqd,bgtd->bgqt", grouped, key_block, preferred_element_type=jnp.float32)
        * scale_factor
    )
    own_scores = (
        jnp.einsum("bgqd,bgd->bgq", grouped, fresh_keys, preferred_element_type=jnp.float32)
        * scale_factor
    )
    live = jnp.arange(key_block.shape[2])[None, :] < live_lengths[:, None]
    weights = jnp.where(live[:, None, None, :], jnp.exp(scores), jnp.float32(0.0))
    own_weight = jnp.exp(own_scores)
    total = jnp.sum(weights, axis=-1) + own_weight
    shares = (weights / total[..., None]).astype(jnp.bfloat16)
    own_share = (own_weight / total).astype(jnp.bfloat16)
    mixed = jnp.einsum("bgqt,bgtd->bgqd", shares, value_block, preferred_element_type=jnp.float32)
    mixed = (
        mixed
        + own_share.astype(jnp.float32)[..., None] * fresh_values.astype(jnp.float32)[:, :, None, :]
    )
    return mixed


def split_kernel(grid, place_ref, rows_ref, *out_refs):
    squares_ref = out_refs[-1]
    step = pl.program_id(0)
    low = place_ref[0]
    block = rows_ref[...]
    wide = block.astype(jnp.float32)

    @pl.when(step == 0)
    def _():
        squares_ref[...] = jnp.zeros_like(squares_ref)

    part = (wide * wide)[:, :LANES]
    for at in range(LANES, wide.shape[1], LANES):
        span = wide[:, at : at + LANES]
        part = part + span * span
    squares_ref[...] += part
    for dg in range(grid.pair):
        half = lax.rem(low + dg, grid.pair)
        start = pl.multiple_of(half * grid.sub, LANES)
        out_refs[dg][...] = rows_ref[:, pl.ds(start, grid.sub)]


def split(grid, rows, low, y_there):
    span_rows, width = rows.shape
    shard = grid.sub * grid.pair
    steps = grid.zs * CORES
    place = jnp.stack([low, y_there]).astype(jnp.int32)

    def column(step, place_ref):
        return (0, ((step // CORES) * grid.ys + place_ref[1]) * CORES + step % CORES)

    piece = jax.ShapeDtypeStruct((span_rows, steps * grid.sub), rows.dtype)
    return pl.pallas_call(
        functools.partial(split_kernel, grid),
        grid_spec=pltpu.PrefetchScalarGridSpec(
            num_scalar_prefetch=1,
            grid=(steps,),
            in_specs=[pl.BlockSpec((span_rows, shard), column)],
            out_specs=[
                pl.BlockSpec((span_rows, grid.sub), lambda step, place_ref: (0, step))
                for _ in range(grid.pair)
            ]
            + [pl.BlockSpec((span_rows, LANES), lambda step, place_ref: (0, 0))],
        ),
        out_shape=[piece] * grid.pair
        + [jax.ShapeDtypeStruct((span_rows, LANES), jnp.float32)],
        name="split",
    )(place, rows)


def product_kernel(grid, order, blocks, place_ref, *refs):
    pieces = len(order)
    acts = refs[:blocks]
    weights = refs[blocks : blocks + pieces]
    outs = refs[blocks + pieces : 2 * blocks + pieces]
    act_store, weight_store, act_sems, weight_sems = refs[2 * blocks + pieces :]
    rows = acts[0].shape[0]
    act_copies = [
        pltpu.make_async_copy(acts[at], act_store.at[pl.ds(at * rows, rows)], act_sems.at[at])
        for at in range(blocks)
    ]
    weight_copies = [
        pltpu.make_async_copy(weights[at], weight_store.at[at], weight_sems.at[at])
        for at in range(pieces)
    ]
    weight_copies[0].start()
    for copy in act_copies:
        copy.start()
    for copy in weight_copies[1:]:
        copy.start()
    for copy in act_copies:
        copy.wait()
    total = None
    for at, (dz, dc) in enumerate(order):
        weight_copies[at].wait()
        z_there = lax.rem(place_ref[0] + grid.zs - dz, grid.zs)
        c_there = lax.rem(place_ref[1] + CORES - dc, CORES)
        start = pl.multiple_of((z_there * CORES + c_there) * grid.sub, LANES)
        term = jnp.dot(
            act_store[:, pl.ds(start, grid.sub)],
            weight_store[at],
            preferred_element_type=jnp.float32,
        )
        total = term if total is None else total + term
    for at in range(blocks):
        outs[at][...] = total[at * rows : (at + 1) * rows].astype(outs[at].dtype)


def product(grid, acts, weights, order, z, c):
    blocks, pieces = len(acts), len(weights)
    rows, depth = acts[0].shape
    width = weights[0].shape[1]
    place = jnp.stack([z, c]).astype(jnp.int32)
    kinds = [jnp.float32] + [jnp.bfloat16] * (blocks - 1)
    anywhere = pl.BlockSpec(memory_space=pl.ANY)
    inside = pl.BlockSpec(memory_space=pltpu.VMEM)
    return pl.pallas_call(
        functools.partial(product_kernel, grid, order, blocks),
        in_specs=[pl.BlockSpec(memory_space=pltpu.SMEM)] + [anywhere] * (blocks + pieces),
        out_specs=[inside] * blocks,
        out_shape=[jax.ShapeDtypeStruct((rows, width), kind) for kind in kinds],
        scratch_shapes=[
            pltpu.VMEM((blocks * rows, depth), acts[0].dtype),
            pltpu.VMEM((pieces,) + weights[0].shape, weights[0].dtype),
            pltpu.SemaphoreType.DMA((blocks,)),
            pltpu.SemaphoreType.DMA((pieces,)),
        ],
        name="product",
    )(place, *acts, *weights)


def per_device(
    grid,
    prompt_rows,
    decode_rows,
    norm_gain,
    w_query,
    w_key,
    w_value,
    key_cache,
    value_cache,
    positions,
    lengths,
    slots,
):
    span_rows, width = prompt_rows.shape
    shard_rows, key_columns = w_key.shape
    kv_heads, head_size = key_cache.shape[1], key_cache.shape[3]
    own_rows = decode_rows.shape[0]
    low = lax.rem(lax.axis_index("grp"), grid.pair)
    me = lax.axis_index("gx")
    z = me // (grid.ys * CORES)
    y = lax.rem(me // CORES, grid.ys)
    c = lax.rem(me, CORES)

    acts, squares = [], None
    for dy in range(grid.ys):
        outs = split(grid, prompt_rows, low, lax.rem(y + dy, grid.ys))
        squares = outs[-1] if squares is None else squares + outs[-1]
        for dg in range(grid.pair):
            acts.append(outs[dg] if dg + dy == 0 else grid.send(outs[dg], dg=dg, dy=dy))

    rows_here = jnp.concatenate([decode_rows, prompt_rows[span_rows - 1 :]], axis=0)
    kinds = own_rows + 1
    normed = normalize(rows_here, norm_gain).reshape(kinds, width // LANES, LANES)
    along_z = jnp.concatenate(
        [normed] + [grid.send(normed, dz=dz) for dz in range(1, grid.zs)], axis=0
    )
    plane = jnp.concatenate(
        [along_z] + [grid.send(along_z, dy=dy) for dy in range(1, grid.ys)], axis=0
    )
    every = jnp.concatenate([plane, grid.send(plane, dc=1)], axis=0)
    every = every.reshape(every.shape[0], width)

    gain_here = lax.dynamic_slice_in_dim(norm_gain, me * shard_rows + low * grid.sub, grid.sub, 0)
    piece = lax.dynamic_slice_in_dim(w_key, low * grid.sub, grid.sub, 0)
    piece = (piece.astype(jnp.float32) * gain_here.astype(jnp.float32)[:, None]).astype(w_key.dtype)
    order, pieces = [], []
    for dz in range(grid.zs):
        here = piece if dz == 0 else grid.send(piece, dz=dz)
        order += [(dz, 0), (dz, 1)]
        pieces += [here, grid.send(here, dc=1)]

    row_ids = jnp.arange(lengths.shape[0], dtype=jnp.int32)
    hit = slots[None, :] == row_ids[:, None]
    span_of = jnp.sum(jnp.where(hit, jnp.arange(slots.shape[0], dtype=jnp.int32)[None, :], 0), axis=1)
    taken = jnp.any(hit, axis=1)
    source = jnp.where(taken, span_of, row_ids // own_rows)
    inner = jnp.where(taken, own_rows, row_ids % own_rows)
    from_c = lax.rem(c - source % CORES + CORES, CORES)
    from_y = lax.rem(y - (source // CORES) % grid.ys + grid.ys, grid.ys)
    from_z = lax.rem(z - source // (CORES * grid.ys) + grid.zs, grid.zs)
    at = ((from_c * grid.ys + from_y) * grid.zs + from_z) * kinds + inner
    pick = (at[:, None] == jnp.arange(every.shape[0], dtype=jnp.int32)[None, :]).astype(jnp.float32)

    query_cos, query_sin = angles_of(lengths, head_size)
    query_sums = jnp.dot(every, w_query, preferred_element_type=jnp.float32)
    query_sums = jnp.dot(pick, query_sums, precision=lax.Precision.HIGHEST)
    total_rows = query_sums.shape[0]
    queries = rotate(query_sums.reshape(total_rows, -1, head_size), query_cos, query_sin)
    queries = queries.reshape(total_rows, -1).astype(jnp.bfloat16)
    features = lax.dynamic_slice_in_dim(every, me * shard_rows, shard_rows, 1)
    fresh = jnp.concatenate(
        [
            jnp.dot(features, w_key, preferred_element_type=jnp.float32),
            jnp.dot(features, w_value, preferred_element_type=jnp.float32),
        ],
        axis=1,
    )
    fresh = jnp.dot(pick, fresh, precision=lax.Precision.HIGHEST).astype(jnp.bfloat16)
    query_columns = queries.shape[1]
    packet = jnp.concatenate([queries, fresh], axis=1).reshape(grid.count, own_rows, -1)
    packet = lax.all_to_all(packet, "gx", split_axis=0, concat_axis=0)

    own_queries = packet[:, :, :query_columns].transpose(1, 0, 2).reshape(own_rows, -1)
    fresh = jnp.sum(packet[:, :, query_columns:].astype(jnp.float32), axis=0)
    own_lengths = lax.dynamic_slice_in_dim(lengths, me * own_rows, own_rows, 0)
    own_cos, own_sin = angles_of(own_lengths, head_size)
    new_keys = rotate(
        fresh[:, :key_columns].reshape(own_rows, kv_heads, head_size), own_cos, own_sin
    ).astype(jnp.bfloat16)
    new_values = fresh[:, key_columns:].reshape(own_rows, kv_heads, head_size).astype(jnp.bfloat16)
    all_heads = own_queries.shape[1] // head_size
    grouped = own_queries.reshape(own_rows, kv_heads, all_heads // kv_heads, head_size)
    mixed = attend(grouped, key_cache, value_cache, new_keys, new_values, own_lengths)
    attended = mixed.reshape(own_rows, all_heads * head_size).astype(jnp.bfloat16)

    partial = product(grid, acts, pieces, order, z, c)
    key_sums = partial[0]
    at = 0
    for dy in range(grid.ys):
        for dg in range(grid.pair):
            if at:
                key_sums = key_sums + grid.send(partial[at], dg=-dg, dy=-dy).astype(jnp.float32)
            at += 1
    square_mean = jnp.sum(squares, axis=1, keepdims=True) / width
    key_sums = key_sums * lax.rsqrt(square_mean + EPSILON)
    cosine, sine = angles_of(positions, head_size)
    prompt_keys = rotate(key_sums.reshape(span_rows, kv_heads, head_size), cosine, sine)
    prompt_keys = prompt_keys.reshape(span_rows, key_columns).astype(jnp.bfloat16)
    return (prompt_keys, attended)


def solution(mesh):
    def run(*args):
        shard_rows = args[4].shape[0] // mesh.shape["gx"]
        grid = Grid(mesh, shard_rows)
        return jax.shard_map(
            functools.partial(per_device, grid),
            mesh=mesh,
            in_specs=(
                P(("grp", "gx"), None),
                P(("grp", "gx"), None),
                P(),
                P(None, "gx"),
                P("gx", None),
                P("gx", None),
                P(("grp", "gx"), None, None, None),
                P(("grp", "gx"), None, None, None),
                P(("grp", "gx")),
                P("grp"),
                P("grp"),
            ),
            out_specs=(P(("grp", "gx"), None), P(("grp", "gx"), None)),
            check_vma=False,
        )(*args)

    return run
```
